32 devices in a mesh: dp: 4 (over y, x), expert: 8 (over z, core).
Axes of the slice: x: 2, y: 2, z: 4, core: 2. Of those that a mesh axis runs over, the one named last changes fastest.
Arguments:
- tokens: bfloat16 [256, 4096], P(('dp', 'expert')), may hold values from -6 to 6
- route_weight: float32 [256, 8], P(('dp', 'expert')), may hold values from 0.1 to 1
- expert_ids: int32 [256, 8], P(('dp', 'expert')), may hold values from 0 to 15, all different within a row; in each aligned block of 8 rows (0 to 7, 8 to 15, ...) at most 8 rows name the same one
- placement: int32 [16], replicated, may hold values from 0 to 15, each once
- pair_step: int32 [8], replicated, may hold values from 0 to 1
- move_slot: int32 [8], replicated, may hold values from 0 to 1
- expert_weights: bfloat16 [16, 3, 4096, 1024], P('expert', None, None, 'dp'), may hold values from -0.375 to 0.375
Outputs:
- mixed: bfloat16 [256, 4096], P(('dp', 'expert'))
- moved_weights: bfloat16 [8, 3, 4096, 1024], P('expert', None, None, 'dp')
The draws below stay inside these ranges and needn't reach their ends.
Inputs may be any that keep to these rules, and one draw needn't show every extreme that they name: `expert_ids`: each row names 8 different experts. Among the rows of one device (aligned blocks of 8 rows, in the order of the tokens) no expert is named more than 8 times, a bound that some block reaches. A permutation of the slots: expert x is held in slot placement[x], which belongs to index placement[x] // 2 of expert.
All inputs are finite; a program needn't handle non-finite values.
Results may differ from the reference program's by a relative error of at most 0.012.
Values may be sent and summed in bfloat16 or wider, within the bound.
A program may use at most 128 MiB of HBM per device.

```python
import math
import jax
import jax.numpy as jnp
import numpy as np
from jax import lax

D = 4096
FF = 1024
TOP = 8
EXP_COL = 2
TOK_DEV = 8
EXPERTS = 16
CAP = 8
TOKENS = 256
N_DP = 4
N_EXPERT = 8


def place_ends(drawn, own_key, least, top_value):
    index_at = [jax.random.randint(jax.random.fold_in(own_key, axis), (), 0, length) for axis, length in enumerate(drawn.shape)]
    longest = drawn.shape.index(max(drawn.shape))
    beside = index_at[:longest] + [(index_at[longest] + 1) % drawn.shape[longest]] + index_at[longest + 1:]
    return drawn.at[tuple(index_at)].set(least).at[tuple(beside)].set(top_value)


def block_scale(key, dims, shards, least, top_value):
    def one(dim, blocks):
        draws = jax.random.uniform(jax.random.fold_in(jax.random.fold_in(key, 6), dim), (blocks,), jnp.float32, least / len(shards), top_value / len(shards))
        return jnp.repeat(jnp.exp(draws), dims[dim] // blocks).reshape((-1,) + (1,) * (len(dims) - dim - 1))

    factor_of = one(*shards[0])
    for cut in shards[1:]:
        factor_of = factor_of * one(*cut)
    return factor_of


def assign_block(rng, own, number, rows, count, top, reach, lean):
    sequence = jax.random.permutation(rng, count)
    heavy_load, ordinary = shares(count, rows * top, reach, lean, True), shares(count, rows * top, reach, lean, False)
    places = jnp.arange(count)

    def named(lengths, rotation):
        used = int((lengths > 0).sum())
        fixed = max(1, used // 4)
        shifted = fixed + (places - fixed + rotation * (used - fixed)) % max(1, count - fixed)
        return jnp.zeros((count,), jnp.int32).at[sequence[jnp.where(places < fixed, places, shifted)]].set(jnp.asarray(lengths, jnp.int32))

    lengths = jnp.where(number % 4 == 0, named(heavy_load, number // 4), named(ordinary, number - number // 4 - 1))
    mixed = jax.random.permutation(jax.random.fold_in(own, 3), count)
    source_of, receiver = mixed[0:count // 2 * 2:2], mixed[1:count // 2 * 2:2]
    margin = jnp.minimum(lengths[source_of] - 1, reach - lengths[receiver]) // 2
    margin = jnp.where((source_of == sequence[0]) | (receiver == sequence[0]) | (lengths[receiver] == 0), 0, jnp.maximum(margin, 0))
    shifted = jax.random.randint(jax.random.fold_in(own, 4), (count // 2,), 0, 1 << 20) % (margin + 1)
    lengths = lengths.at[source_of].add(-shifted).at[receiver].add(shifted)
    members = jnp.searchsorted(jnp.cumsum(lengths), jnp.arange(rows * top), side="right").astype(jnp.int32)
    grid = members.reshape(top, rows).T
    grid = grid[jax.random.permutation(jax.random.fold_in(own, 1), rows)]
    rotation = jax.random.randint(jax.random.fold_in(own, 2), (rows, 1), 0, top)
    return jnp.take_along_axis(grid, (jnp.arange(top)[None, :] + rotation) % top, axis=1)


def shares(number_of, total, bound, lean, full):
    loads = [(1 << 20) // math.isqrt(grade ** lean) + 1 for grade in range(1, number_of + 1)]
    largest = bound if full else min(bound, max(-(-total // number_of), total * loads[0] // sum(loads)))
    least = 1 if total - largest >= number_of - 1 else 0
    given, rest = [largest] + [least] * (number_of - 1), total - largest - least * (number_of - 1)
    while rest > 0:
        candidates = [i for i in range(1, number_of) if given[i] < largest] or [i for i in range(1, number_of) if given[i] < bound]
        whole, left = sum([loads[i] for i in candidates]), rest
        for i in candidates:
            more = min(bound - given[i], max(1, left * loads[i] // whole), rest)
            given[i] = given[i] + more
            rest = rest - more
    return np.array(given)


def normal_values(key, dims, deviation, most, split=(), held_as=jnp.bfloat16):
    array = deviation * jax.random.normal(key, dims, jnp.float32)
    if split:
        array = array * block_scale(key, dims, split, -0.22, 0.18)
    return jnp.clip(array, -most, most).astype(held_as)


def setup_inputs(seed: int = 0) -> dict:
    keys = jax.random.split(jax.random.key(seed), 8)
    tokens = normal_values(keys[0], (TOKENS, D), 1.0, 6.0, ((0, 32),))
    route_weight = jnp.clip(0.1 + 0.9 * jax.random.uniform(keys[1], (TOKENS, TOP), jnp.float32) ** block_scale(keys[1], (TOKENS, TOP), ((0, 32),), -0.2, 0.2), 0.1, 1.0)
    expert_ids_keys = jax.random.split(jax.random.fold_in(keys[2], 1), TOKENS // TOK_DEV)
    expert_ids_turns = jax.random.permutation(jax.random.fold_in(keys[2], 3), TOKENS // TOK_DEV)
    expert_ids = jax.vmap(lambda own, number: assign_block(jax.random.fold_in(keys[2], 2), own, number, TOK_DEV, EXPERTS, TOP, CAP, 2))(expert_ids_keys, expert_ids_turns).reshape((TOKENS, TOP))
    placement = jax.random.permutation(keys[3], EXPERTS).astype(jnp.int32)
    pair_step = place_ends(jax.random.randint(keys[4], (N_EXPERT,), 0, 2), jax.random.fold_in(keys[4], 1), 0, 1).astype(jnp.int32)
    move_slot = place_ends(jax.random.randint(keys[5], (N_EXPERT,), 0, EXP_COL), jax.random.fold_in(keys[5], 1), 0, EXP_COL - 1).astype(jnp.int32)
    expert_weights = normal_values(keys[6], (EXPERTS, 3, D, FF), (1.5 * D ** -0.5), 0.375, ((0, 8), (3, 4)))
    return dict(tokens=tokens, route_weight=route_weight, expert_ids=expert_ids, placement=placement, pair_step=pair_step, move_slot=move_slot, expert_weights=expert_weights)


def pair_offsets(flags):
    count = flags.shape[0]
    columns = jnp.arange(count, dtype=jnp.int32)
    joined = jnp.repeat(jnp.sum(flags.reshape(-1, 2), axis=1) > 0, 2)
    return jnp.where(joined, 1 - 2 * (columns % 2), 0).astype(jnp.int32)


def reference(tokens, route_weight, expert_ids, placement, pair_step, move_slot, expert_weights):
    columns = jnp.arange(N_EXPERT, dtype=jnp.int32)
    source = (columns + pair_offsets(pair_step)).astype(jnp.int32)
    src_slot = (source * EXP_COL + move_slot[source]).astype(jnp.int32)
    moved_weights = expert_weights[src_slot]
    flat_ids = expert_ids.reshape(-1).astype(jnp.int32)
    matches = (flat_ids[:, None] == jnp.arange(EXPERTS, dtype=jnp.int32)[None, :]).astype(jnp.int32)
    position = jnp.sum(matches * (jnp.cumsum(matches, axis=0) - 1), axis=1).astype(jnp.int32)
    rows_per = (TOKENS // TOK_DEV) * CAP
    token_of = jnp.arange(TOKENS * TOP, dtype=jnp.int32) // TOP
    buffer = jnp.zeros((EXPERTS, rows_per, D), jnp.bfloat16).at[flat_ids, position].set(tokens[token_of])

    def one_expert(pair_in):
        row_data, expert_index = pair_in
        weights = lax.dynamic_index_in_dim(expert_weights, placement[expert_index], 0, keepdims=False)
        gate_act = jnp.dot(row_data, weights[0], preferred_element_type=jnp.float32)
        up_act = jnp.dot(row_data, weights[1], preferred_element_type=jnp.float32)
        hidden = (jax.nn.silu(gate_act) * up_act).astype(jnp.bfloat16)
        grouped = hidden.reshape(rows_per, N_DP, FF // N_DP).astype(jnp.float32)
        down_weight = weights[2].reshape(D, N_DP, FF // N_DP).astype(jnp.float32)
        partial_value = jnp.einsum("rgh,dgh->rgd", grouped, down_weight).astype(jnp.bfloat16)
        partial_value = lax.optimization_barrier(partial_value).astype(jnp.float32)
        return jnp.sum(partial_value, axis=1).astype(jnp.bfloat16)

    outputs = lax.map(one_expert, (buffer, jnp.arange(EXPERTS, dtype=jnp.int32)))
    picked = outputs[flat_ids, position].reshape(TOKENS, TOP, D).astype(jnp.float32)
    mixed = jnp.sum(route_weight[:, :, None] * picked, axis=1).astype(jnp.bfloat16)
    return mixed, moved_weights
```

```python
import functools

import jax
import jax.numpy as jnp
from jax import lax
from jax.experimental import pallas as pl
from jax.experimental.pallas import tpu as pltpu
from jax.sharding import PartitionSpec as P

MESH = pl.DeviceIdType.MESH
LANES = 128
VMEM_LIMIT = 56 * 1024 * 1024


def place(nd, nz):
    d = lax.axis_index("dp")
    e = lax.axis_index("expert")
    return d, e // 2, e % 2, e


def enter(nd, nz, d, zz, c, e):
    barrier = pltpu.get_barrier_semaphore()
    peers = [(d, zz * 2 + 1 - c)]
    peers += [(lax.rem(d + k, nd), e) for k in range(1, nd)]
    peers += [(d, lax.rem(zz + i, nz) * 2 + c) for i in range(1, nz)]
    for pd, pe in peers:
        pl.semaphore_signal(barrier, inc=1, device_id={"dp": pd, "expert": pe}, device_id_type=MESH)
    pl.semaphore_wait(barrier, len(peers))


def remote(src, dst, send, recv, pd, pe):
    return pltpu.make_async_remote_copy(
        src_ref=src,
        dst_ref=dst,
        send_sem=send,
        recv_sem=recv,
        device_id={"dp": pd, "expert": pe},
        device_id_type=MESH,
    )


def gather_kernel(
    nd, nz, mv_ref, msg_ref, w_hbm, g_ref, got_hbm,
    out_ref, w_sem, a_send, a_recv, b_send, b_recv, c_send, c_recv, s_send, s_recv, *w_refs,
):
    d, zz, c, e = place(nd, nz)
    sibling = zz * 2 + 1 - c
    slots, parts, rows, _ = w_hbm.shape
    loads = [
        [pltpu.make_async_copy(w_hbm.at[j, m], w_refs[m].at[j], w_sem.at[j, m]) for j in range(slots)]
        for m in range(parts)
    ]
    for part in loads:
        for load in part:
            load.start()
    g_ref[c, zz, d] = msg_ref[...]
    enter(nd, nz, d, zz, c, e)
    started = []
    for i in range(1, nz):
        block = g_ref.at[c, zz, d]
        copy = remote(block, block, a_send.at[i - 1], a_recv.at[i - 1], d, lax.rem(zz + i, nz) * 2 + c)
        copy.start()
        started.append(copy)

    def to_dp(i):
        block = g_ref.at[c, lax.rem(zz - i + nz, nz), d]
        for k in range(1, nd):
            copy = remote(block, block, b_send.at[i, k - 1], b_recv.at[i, k - 1], lax.rem(d + k, nd), e)
            copy.start()
            started.append(copy)

    to_dp(0)
    moving = mv_ref[0]
    tile = min(rows, 256)

    def swap(m):
        for load in loads[m]:
            load.wait()

        def step(r, carry):
            at = pl.ds(pl.multiple_of(r * tile, tile), tile)
            out_ref[m, at, :] = w_refs[m][moving, at, :]
            return carry

        lax.fori_loop(0, rows // tile, step, 0)
        copy = remote(out_ref.at[m], got_hbm.at[m], s_send.at[m], s_recv.at[m], d, sibling)
        copy.start()
        started.append(copy)
        return copy

    swaps = [swap(0)]
    for i in range(1, nz):
        block = g_ref.at[c, lax.rem(zz - i + nz, nz), d]
        remote(block, block, a_send.at[i - 1], a_recv.at[i - 1], d, e).wait_recv()
        to_dp(i)
    for m in range(1, parts):
        swaps.append(swap(m))
    groups = []
    for i in range(nz):
        at = lax.rem(zz - i + nz, nz)
        for k in range(1, nd):
            block = g_ref.at[c, at, lax.rem(d - k + nd, nd)]
            remote(block, block, b_send.at[i, k - 1], b_recv.at[i, k - 1], d, e).wait_recv()
        copy = remote(g_ref.at[c, at], g_ref.at[c, at], c_send.at[i], c_recv.at[i], d, sibling)
        copy.start()
        started.append(copy)
        groups.append(copy)
    for copy in groups + swaps:
        copy.wait_recv()
    for copy in started:
        copy.wait_send()


def expert_kernel(flag_ref, g_ref, w_hbm, got_hbm, p_ref, moved_hbm, w_ref, x_ref, h_ref, w_sem, m_sem):
    blocks, rows_of, _ = g_ref.shape
    slots, parts, width, hidden = w_hbm.shape
    lanes = (g_ref.shape[2] - width) // 2
    chunk = min(width, 1024)
    chunks = width // chunk
    e = lax.axis_index("expert")

    def load(j, m, q):
        at = pl.ds(q * chunk, chunk)
        return pltpu.make_async_copy(w_hbm.at[j, m, at], w_ref.at[j, m, at], w_sem.at[j, m, q])

    order = [(j, m, q) for j in range(slots) for q in range(chunks) for m in (0, 1)]
    order += [(j, 2, q) for q in range(chunks) for j in range(slots)]
    for key in order:
        load(*key).start()
    swapping = flag_ref[0] != 0

    @pl.when(swapping)
    def _():
        pltpu.make_async_copy(got_hbm, moved_hbm.at[0], m_sem).start()

    @pl.when(jnp.logical_not(swapping))
    def _():
        pltpu.make_async_copy(w_hbm.at[flag_ref[1]], moved_hbm.at[0], m_sem).start()

    per = min(blocks, max(1, 256 // rows_of))
    rows = per * rows_of

    def tile(t, waiting):
        at = pl.ds(t * per, per)
        x_ref[...] = g_ref[at, :, :width].astype(jnp.float32).reshape(rows, width).astype(jnp.bfloat16)
        share = (
            g_ref[at, :, width : width + lanes].astype(jnp.float32)
            + g_ref[at, :, width + lanes :].astype(jnp.float32)
        ).reshape(rows, lanes)
        lane = lax.broadcasted_iota(jnp.int32, (rows, lanes), 1)
        for j in range(slots):
            weight = jnp.sum(jnp.where(lane == e * slots + j, share, 0.0), axis=1, keepdims=True)
            gate = jnp.zeros((rows, hidden), jnp.float32)
            up = jnp.zeros((rows, hidden), jnp.float32)
            for q in range(chunks):
                cut = pl.ds(q * chunk, chunk)
                if waiting:
                    load(j, 0, q).wait()
                    load(j, 1, q).wait()
                x = x_ref[:, cut]
                gate += jnp.dot(x, w_ref[j, 0, cut, :], preferred_element_type=jnp.float32)
                up += jnp.dot(x, w_ref[j, 1, cut, :], preferred_element_type=jnp.float32)
            value = weight * (gate / (1.0 + jnp.exp(-gate)) * up)
            h_ref[:, pl.ds(j * hidden, hidden)] = value.astype(jnp.bfloat16)
        for q in range(chunks):
            cut = pl.ds(q * chunk, chunk)
            total = jnp.zeros((rows, chunk), jnp.float32)
            for j in range(slots):
                if waiting:
                    load(j, 2, q).wait()
                total += lax.dot_general(
                    h_ref[:, pl.ds(j * hidden, hidden)],
                    w_ref[j, 2, cut, :],
                    (((1,), (1,)), ((), ())),
                    preferred_element_type=jnp.float32,
                )
            p_ref[at, :, cut] = total.reshape(per, rows_of, chunk).astype(jnp.bfloat16)

    tile(0, True)
    if blocks > per:
        def step(t, carry):
            tile(t, False)
            return carry

        lax.fori_loop(1, blocks // per, step, 0)
    pltpu.make_async_copy(got_hbm, moved_hbm.at[0], m_sem).wait()


def scatter_kernel(
    nd, nz, p_ref, y_ref, rc_ref, s1_ref, rb_ref, s2_ref, ra_ref,
    a_send, a_recv, b_send, b_recv, c_send, c_recv,
):
    d, zz, c, e = place(nd, nz)
    sibling = zz * 2 + 1 - c
    f32 = jnp.float32
    enter(nd, nz, d, zz, c, e)
    started = []
    order = list(range(1, nz)) + [0]
    for i in order:
        at = lax.rem(zz + i, nz)
        copy = remote(p_ref.at[1 - c, at], rc_ref.at[i], c_send.at[i], c_recv.at[i], d, sibling)
        copy.start()
        started.append(copy)
    for i in order:
        at = lax.rem(zz + i, nz)
        remote(p_ref.at[1 - c, at], rc_ref.at[i], c_send.at[i], c_recv.at[i], d, sibling).wait_recv()
        for k in list(range(1, nd)) + [0]:
            pd = lax.rem(d + k, nd)
            s1_ref[i, k] = (p_ref[c, at, pd].astype(f32) + rc_ref[i, pd].astype(f32)).astype(jnp.bfloat16)
            if k:
                copy = remote(s1_ref.at[i, k], rb_ref.at[i, k - 1], b_send.at[i, k - 1], b_recv.at[i, k - 1], pd, e)
                copy.start()
                started.append(copy)
    final = None
    for i in order:
        total = s1_ref[i, 0].astype(f32)
        for k in range(1, nd):
            remote(s1_ref.at[i, k], rb_ref.at[i, k - 1], b_send.at[i, k - 1], b_recv.at[i, k - 1], d, e).wait_recv()
            total += rb_ref[i, k - 1].astype(f32)
        if i:
            s2_ref[i - 1] = total.astype(jnp.bfloat16)
            pe = lax.rem(zz + i, nz) * 2 + c
            copy = remote(s2_ref.at[i - 1], ra_ref.at[i - 1], a_send.at[i - 1], a_recv.at[i - 1], d, pe)
            copy.start()
            started.append(copy)
        else:
            final = total
    for i in range(1, nz):
        remote(s2_ref.at[i - 1], ra_ref.at[i - 1], a_send.at[i - 1], a_recv.at[i - 1], d, e).wait_recv()
        final += ra_ref[i - 1].astype(f32)
    y_ref[...] = final.astype(jnp.bfloat16)
    for copy in started:
        copy.wait_send()


def message(tokens, route_weight, expert_ids, placement):
    experts = placement.shape[0]
    lanes = -(-experts // LANES) * LANES
    names = jnp.arange(experts, dtype=jnp.int32)
    chosen = jnp.sum(
        jnp.where(expert_ids[:, :, None] == names[None, None, :], route_weight[:, :, None], 0.0), axis=1
    )
    slots = jnp.arange(lanes, dtype=jnp.int32)
    share = jnp.sum(
        jnp.where(placement[None, :, None] == slots[None, None, :], chosen[:, :, None], 0.0), axis=1
    )
    high = lax.reduce_precision(share, 8, 7)
    low = share - high
    return jnp.concatenate([tokens, high.astype(jnp.bfloat16), low.astype(jnp.bfloat16)], axis=1)


def body(tokens, route_weight, expert_ids, placement, pair_step, move_slot, expert_weights):
    nd = lax.axis_size("dp")
    nz = lax.axis_size("expert") // 2
    e = lax.axis_index("expert")
    rows, width = tokens.shape
    slots, parts, _, hidden = expert_weights.shape
    bf16 = jnp.bfloat16
    vmem = pl.BlockSpec(memory_space=pltpu.VMEM)
    smem = pl.BlockSpec(memory_space=pltpu.SMEM)
    anywhere = pl.BlockSpec(memory_space=pl.ANY)
    dma = pltpu.SemaphoreType.DMA

    steps = pair_step.reshape(-1, 2).sum(axis=1)
    swap_here = (lax.dynamic_index_in_dim(steps, e // 2, 0, keepdims=False) > 0).astype(jnp.int32)
    moving = lax.dynamic_index_in_dim(move_slot, e, 0, keepdims=False)
    flags = jnp.stack([swap_here, moving])
    msg = message(tokens, route_weight, expert_ids, placement)
    full = msg.shape[1]

    gathered, got = pl.pallas_call(
        functools.partial(gather_kernel, nd, nz),
        out_shape=(
            jax.ShapeDtypeStruct((2, nz, nd, rows, full), bf16),
            jax.ShapeDtypeStruct((parts, width, hidden), bf16),
        ),
        in_specs=[smem, vmem, anywhere],
        out_specs=(vmem, anywhere),
        scratch_shapes=[
            pltpu.VMEM((parts, width, hidden), bf16),
            dma((slots, parts)),
            dma((nz - 1,)), dma((nz - 1,)),
            dma((nz, nd - 1)), dma((nz, nd - 1)),
            dma((nz,)), dma((nz,)),
            dma((parts,)), dma((parts,)),
        ] + [pltpu.VMEM((slots, width, hidden), bf16)] * parts,
        compiler_params=pltpu.CompilerParams(
            collective_id=0, has_side_effects=True, vmem_limit_bytes=VMEM_LIMIT
        ),
        name="gather",
    )(moving[None], msg, expert_weights)

    blocks = 2 * nz * nd
    per = min(blocks, max(1, 256 // rows))
    chunks = width // min(width, 1024)
    partial, moved = pl.pallas_call(
        expert_kernel,
        out_shape=(
            jax.ShapeDtypeStruct((blocks, rows, width), bf16),
            jax.ShapeDtypeStruct((1, parts, width, hidden), bf16),
        ),
        in_specs=[smem, vmem, anywhere, anywhere],
        out_specs=(vmem, anywhere),
        scratch_shapes=[
            pltpu.VMEM((slots, parts, width, hidden), bf16),
            pltpu.VMEM((per * rows, width), bf16),
            pltpu.VMEM((per * rows, slots * hidden), bf16),
            dma((slots, parts, chunks)),
            dma,
        ],
        compiler_params=pltpu.CompilerParams(vmem_limit_bytes=VMEM_LIMIT),
        name="experts",
    )(flags, gathered.reshape(blocks, rows, full), expert_weights, got)

    mixed = pl.pallas_call(
        functools.partial(scatter_kernel, nd, nz),
        out_shape=jax.ShapeDtypeStruct((rows, width), bf16),
        in_specs=[vmem],
        out_specs=vmem,
        scratch_shapes=[
            pltpu.VMEM((nz, nd, rows, width), bf16),
            pltpu.VMEM((nz, nd, rows, width), bf16),
            pltpu.VMEM((nz, nd - 1, rows, width), bf16),
            pltpu.VMEM((nz - 1, rows, width), bf16),
            pltpu.VMEM((nz - 1, rows, width), bf16),
            dma((nz - 1,)), dma((nz - 1,)),
            dma((nz, nd - 1)), dma((nz, nd - 1)),
            dma((nz,)), dma((nz,)),
        ],
        compiler_params=pltpu.CompilerParams(
            collective_id=1, has_side_effects=True, vmem_limit_bytes=VMEM_LIMIT
        ),
        name="scatter",
    )(partial.reshape(2, nz, nd, rows, width))
    return mixed, moved


def solution(mesh):
    in_specs = (
        P(("dp", "expert"), None),
        P(("dp", "expert"), None),
        P(("dp", "expert"), None),
        P(),
        P(),
        P(),
        P("expert", None, None, "dp"),
    )
    out_specs = (P(("dp", "expert"), None), P("expert", None, None, "dp"))
    return jax.shard_map(body, mesh=mesh, in_specs=in_specs, out_specs=out_specs, check_vma=False)
```

```python
import functools

import jax
import jax.numpy as jnp
from jax import lax
from jax.experimental import pallas as pl
from jax.experimental.pallas import tpu as pltpu
from jax.sharding import PartitionSpec as P

MESH = pl.DeviceIdType.MESH
LANES = 128
VMEM_LIMIT = 56 * 1024 * 1024


def place(nd, nz):
    d = lax.axis_index("dp")
    e = lax.axis_index("expert")
    return d, e // 2, e % 2, e


def enter(nd, nz, d, zz, c, e):
    barrier = pltpu.get_barrier_semaphore()
    peers = [(d, zz * 2 + 1 - c)]
    peers += [(lax.rem(d + k, nd), e) for k in range(1, nd)]
    peers += [(d, lax.rem(zz + i, nz) * 2 + c) for i in range(1, nz)]
    for pd, pe in peers:
        pl.semaphore_signal(barrier, inc=1, device_id={"dp": pd, "expert": pe}, device_id_type=MESH)
    pl.semaphore_wait(barrier, len(peers))


def remote(src, dst, send, recv, pd, pe):
    return pltpu.make_async_remote_copy(
        src_ref=src,
        dst_ref=dst,
        send_sem=send,
        recv_sem=recv,
        device_id={"dp": pd, "expert": pe},
        device_id_type=MESH,
    )


def gather_kernel(
    nd, nz, mv_ref, x_ref, rw_ref, id_ref, w_hbm, g_ref, got_hbm,
    out_ref, w_sem, a_send, a_recv, b_send, b_recv, c_send, c_recv, s_send, s_recv, *w_refs,
):
    d, zz, c, e = place(nd, nz)
    sibling = zz * 2 + 1 - c
    slots, parts, rows, _ = w_hbm.shape
    loads = [
        [pltpu.make_async_copy(w_hbm.at[j, m], w_refs[m].at[j], w_sem.at[j, m]) for j in range(slots)]
        for m in range(parts)
    ]
    for part in loads:
        for load in part:
            load.start()
    width = x_ref.shape[1]
    lanes = (g_ref.shape[4] - width) // 2
    lane = lax.broadcasted_iota(jnp.int32, (x_ref.shape[0], lanes), 1)
    share = jnp.zeros(lane.shape, jnp.float32)
    for k in range(id_ref.shape[1]):
        share += jnp.where(lane == id_ref[:, k : k + 1], rw_ref[:, k : k + 1], 0.0)
    high = share.astype(jnp.bfloat16)
    g_ref[c, zz, d, :, :width] = x_ref[...]
    g_ref[c, zz, d, :, width : width + lanes] = high
    g_ref[c, zz, d, :, width + lanes :] = (share - high.astype(jnp.float32)).astype(jnp.bfloat16)
    enter(nd, nz, d, zz, c, e)
    started = []
    for i in range(1, nz):
        block = g_ref.at[c, zz, d]
        copy = remote(block, block, a_send.at[i - 1], a_recv.at[i - 1], d, lax.rem(zz + i, nz) * 2 + c)
        copy.start()
        started.append(copy)

    def to_dp(i):
        block = g_ref.at[c, lax.rem(zz - i + nz, nz), d]
        for k in range(1, nd):
            copy = remote(block, block, b_send.at[i, k - 1], b_recv.at[i, k - 1], lax.rem(d + k, nd), e)
            copy.start()
            started.append(copy)

    to_dp(0)
    moving = mv_ref[e]
    tile = min(rows, 256)

    def swap(m):
        for load in loads[m]:
            load.wait()

        def step(r, carry):
            at = pl.ds(pl.multiple_of(r * tile, tile), tile)
            out_ref[m, at, :] = w_refs[m][moving, at, :]
            return carry

        lax.fori_loop(0, rows // tile, step, 0)
        copy = remote(out_ref.at[m], got_hbm.at[m], s_send.at[m], s_recv.at[m], d, sibling)
        copy.start()
        started.append(copy)
        return copy

    swaps = [swap(0)]
    for i in range(1, nz):
        block = g_ref.at[c, lax.rem(zz - i + nz, nz), d]
        remote(block, block, a_send.at[i - 1], a_recv.at[i - 1], d, e).wait_recv()
        to_dp(i)
    for m in range(1, parts):
        swaps.append(swap(m))
    groups = []
    for i in range(nz):
        at = lax.rem(zz - i + nz, nz)
        for k in range(1, nd):
            block = g_ref.at[c, at, lax.rem(d - k + nd, nd)]
            remote(block, block, b_send.at[i, k - 1], b_recv.at[i, k - 1], d, e).wait_recv()
        copy = remote(g_ref.at[c, at], g_ref.at[c, at], c_send.at[i], c_recv.at[i], d, sibling)
        copy.start()
        started.append(copy)
        groups.append(copy)
    for copy in groups + swaps:
        copy.wait_recv()
    for copy in started:
        copy.wait_send()


def expert_kernel(
    place_ref, step_ref, mv_ref, g_ref, w_hbm, got_hbm, p_ref, moved_hbm,
    w_ref, x_ref, h_ref, m_ref, w_sem, m_sem, o_sem,
):
    blocks, rows_of, _ = g_ref.shape
    slots, parts, width, hidden = w_hbm.shape
    lanes = (g_ref.shape[2] - width) // 2
    chunk = min(width, 1024)
    chunks = width // chunk
    e = lax.axis_index("expert")

    def load(j, m, q):
        at = pl.ds(q * chunk, chunk)
        return pltpu.make_async_copy(w_hbm.at[j, m, at], w_ref.at[j, m, at], w_sem.at[j, m, q])

    order = [(j, m, q) for j in range(slots) for q in range(chunks) for m in (0, 1)]
    order += [(j, 2, q) for q in range(chunks) for j in range(slots)]
    for key in order:
        load(*key).start()
    first = e // 2 * 2
    swapping = step_ref[first] + step_ref[first + 1] > 0

    @pl.when(swapping)
    def _():
        for m in range(parts):
            pltpu.make_async_copy(got_hbm.at[m], m_ref.at[m], m_sem.at[m]).start()

    @pl.when(jnp.logical_not(swapping))
    def _():
        for m in range(parts):
            pltpu.make_async_copy(w_hbm.at[mv_ref[e], m], m_ref.at[m], m_sem.at[m]).start()

    def put(m):
        return pltpu.make_async_copy(m_ref.at[m], moved_hbm.at[0, m], o_sem.at[m])

    def put_all():
        for m in range(parts):
            pltpu.make_async_copy(got_hbm.at[m], m_ref.at[m], m_sem.at[m]).wait()
            put(m).start()

    per = min(blocks, max(1, 256 // rows_of))
    rows = per * rows_of

    def tile(t, waiting):
        at = pl.ds(t * per, per)
        x_ref[...] = g_ref[at, :, :width].astype(jnp.float32).reshape(rows, width).astype(jnp.bfloat16)
        share = (
            g_ref[at, :, width : width + lanes].astype(jnp.float32)
            + g_ref[at, :, width + lanes :].astype(jnp.float32)
        ).reshape(rows, lanes)
        lane = lax.broadcasted_iota(jnp.int32, (1, lanes), 1)
        held = jnp.full((1, lanes), -1, jnp.int32)
        for name in range(place_ref.shape[0]):
            held = jnp.where(lane == name, place_ref[name], held)
        for j in range(slots):
            weight = jnp.sum(jnp.where(held == e * slots + j, share, 0.0), axis=1, keepdims=True)
            gate = jnp.zeros((rows, hidden), jnp.float32)
            up = jnp.zeros((rows, hidden), jnp.float32)
            for q in range(chunks):
                cut = pl.ds(q * chunk, chunk)
                if waiting:
                    load(j, 0, q).wait()
                    load(j, 1, q).wait()
                x = x_ref[:, cut]
                gate += jnp.dot(x, w_ref[j, 0, cut, :], preferred_element_type=jnp.float32)
                up += jnp.dot(x, w_ref[j, 1, cut, :], preferred_element_type=jnp.float32)
            value = weight * (gate / (1.0 + jnp.exp(-gate)) * up)
            h_ref[:, pl.ds(j * hidden, hidden)] = value.astype(jnp.bfloat16)
        for q in range(chunks):
            if waiting and q == chunks // 2:
                put_all()
            cut = pl.ds(q * chunk, chunk)
            total = jnp.zeros((rows, chunk), jnp.float32)
            for j in range(slots):
                if waiting:
                    load(j, 2, q).wait()
                total += lax.dot_general(
                    h_ref[:, pl.ds(j * hidden, hidden)],
                    w_ref[j, 2, cut, :],
                    (((1,), (1,)), ((), ())),
                    preferred_element_type=jnp.float32,
                )
            p_ref[at, :, cut] = total.reshape(per, rows_of, chunk).astype(jnp.bfloat16)

    tile(0, True)
    if blocks > per:
        def step(t, carry):
            tile(t, False)
            return carry

        lax.fori_loop(1, blocks // per, step, 0)
    for m in range(parts):
        put(m).wait()


def scatter_kernel(
    nd, nz, p_ref, y_ref, rc_ref, s1_ref, rb_ref, s2_ref, ra_ref,
    a_send, a_recv, b_send, b_recv, c_send, c_recv,
):
    d, zz, c, e = place(nd, nz)
    sibling = zz * 2 + 1 - c
    f32 = jnp.float32
    enter(nd, nz, d, zz, c, e)
    started = []
    order = list(range(1, nz)) + [0]
    for i in order:
        at = lax.rem(zz + i, nz)
        copy = remote(p_ref.at[1 - c, at], rc_ref.at[i], c_send.at[i], c_recv.at[i], d, sibling)
        copy.start()
        started.append(copy)
    for i in order:
        at = lax.rem(zz + i, nz)
        remote(p_ref.at[1 - c, at], rc_ref.at[i], c_send.at[i], c_recv.at[i], d, sibling).wait_recv()
        for k in list(range(1, nd)) + [0]:
            pd = lax.rem(d + k, nd)
            s1_ref[i, k] = (p_ref[c, at, pd].astype(f32) + rc_ref[i, pd].astype(f32)).astype(jnp.bfloat16)
            if k:
                copy = remote(s1_ref.at[i, k], rb_ref.at[i, k - 1], b_send.at[i, k - 1], b_recv.at[i, k - 1], pd, e)
                copy.start()
                started.append(copy)
    final = None
    for i in order:
        total = s1_ref[i, 0].astype(f32)
        for k in range(1, nd):
            remote(s1_ref.at[i, k], rb_ref.at[i, k - 1], b_send.at[i, k - 1], b_recv.at[i, k - 1], d, e).wait_recv()
            total += rb_ref[i, k - 1].astype(f32)
        if i:
            s2_ref[i - 1] = total.astype(jnp.bfloat16)
            pe = lax.rem(zz + i, nz) * 2 + c
            copy = remote(s2_ref.at[i - 1], ra_ref.at[i - 1], a_send.at[i - 1], a_recv.at[i - 1], d, pe)
            copy.start()
            started.append(copy)
        else:
            final = total
    for i in range(1, nz):
        remote(s2_ref.at[i - 1], ra_ref.at[i - 1], a_send.at[i - 1], a_recv.at[i - 1], d, e).wait_recv()
        final += ra_ref[i - 1].astype(f32)
    y_ref[...] = final.astype(jnp.bfloat16)
    for copy in started:
        copy.wait_send()


def body(tokens, route_weight, expert_ids, placement, pair_step, move_slot, expert_weights):
    nd = lax.axis_size("dp")
    nz = lax.axis_size("expert") // 2
    e = lax.axis_index("expert")
    rows, width = tokens.shape
    slots, parts, _, hidden = expert_weights.shape
    bf16 = jnp.bfloat16
    vmem = pl.BlockSpec(memory_space=pltpu.VMEM)
    smem = pl.BlockSpec(memory_space=pltpu.SMEM)
    anywhere = pl.BlockSpec(memory_space=pl.ANY)
    dma = pltpu.SemaphoreType.DMA

    experts = placement.shape[0]
    full = width + 2 * (-(-experts // LANES) * LANES)

    gathered, got = pl.pallas_call(
        functools.partial(gather_kernel, nd, nz),
        out_shape=(
            jax.ShapeDtypeStruct((2, nz, nd, rows, full), bf16),
            jax.ShapeDtypeStruct((parts, width, hidden), bf16),
        ),
        in_specs=[smem, vmem, vmem, vmem, anywhere],
        out_specs=(vmem, anywhere),
        scratch_shapes=[
            pltpu.VMEM((parts, width, hidden), bf16),
            dma((slots, parts)),
            dma((nz - 1,)), dma((nz - 1,)),
            dma((nz, nd - 1)), dma((nz, nd - 1)),
            dma((nz,)), dma((nz,)),
            dma((parts,)), dma((parts,)),
        ] + [pltpu.VMEM((slots, width, hidden), bf16)] * parts,
        compiler_params=pltpu.CompilerParams(
            collective_id=0, has_side_effects=True, vmem_limit_bytes=VMEM_LIMIT
        ),
        name="gather",
    )(move_slot, tokens, route_weight, expert_ids, expert_weights)

    blocks = 2 * nz * nd
    per = min(blocks, max(1, 256 // rows))
    chunks = width // min(width, 1024)
    partial, moved = pl.pallas_call(
        expert_kernel,
        out_shape=(
            jax.ShapeDtypeStruct((blocks, rows, width), bf16),
            jax.ShapeDtypeStruct((1, parts, width, hidden), bf16),
        ),
        in_specs=[smem, smem, smem, vmem, anywhere, anywhere],
        out_specs=(vmem, anywhere),
        scratch_shapes=[
            pltpu.VMEM((slots, parts, width, hidden), bf16),
            pltpu.VMEM((per * rows, width), bf16),
            pltpu.VMEM((per * rows, slots * hidden), bf16),
            pltpu.VMEM((parts, width, hidden), bf16),
            dma((slots, parts, chunks)),
            dma((parts,)),
            dma((parts,)),
        ],
        compiler_params=pltpu.CompilerParams(vmem_limit_bytes=VMEM_LIMIT),
        name="experts",
    )(placement, pair_step, move_slot, gathered.reshape(blocks, rows, full), expert_weights, got)

    mixed = pl.pallas_call(
        functools.partial(scatter_kernel, nd, nz),
        out_shape=jax.ShapeDtypeStruct((rows, width), bf16),
        in_specs=[vmem],
        out_specs=vmem,
        scratch_shapes=[
            pltpu.VMEM((nz, nd, rows, width), bf16),
            pltpu.VMEM((nz, nd, rows, width), bf16),
            pltpu.VMEM((nz, nd - 1, rows, width), bf16),
            pltpu.VMEM((nz - 1, rows, width), bf16),
            pltpu.VMEM((nz - 1, rows, width), bf16),
            dma((nz - 1,)), dma((nz - 1,)),
            dma((nz, nd - 1)), dma((nz, nd - 1)),
            dma((nz,)), dma((nz,)),
        ],
        compiler_params=pltpu.CompilerParams(
            collective_id=1, has_side_effects=True, vmem_limit_bytes=VMEM_LIMIT
        ),
        name="scatter",
    )(partial.reshape(2, nz, nd, rows, width))
    return mixed, moved


def solution(mesh):
    in_specs = (
        P(("dp", "expert"), None),
        P(("dp", "expert"), None),
        P(("dp", "expert"), None),
        P(),
        P(),
        P(),
        P("expert", None, None, "dp"),
    )
    out_specs = (P(("dp", "expert"), None), P("expert", None, None, "dp"))
    return jax.shard_map(body, mesh=mesh, in_specs=in_specs, out_specs=out_specs, check_vma=False)
```

```python
import functools

import jax
import jax.numpy as jnp
from jax import lax
from jax.experimental import pallas as pl
from jax.experimental.pallas import tpu as pltpu
from jax.sharding import PartitionSpec as P

MESH = pl.DeviceIdType.MESH
LANES = 128
VMEM_LIMIT = 56 * 1024 * 1024


def place(nd, nz):
    d = lax.axis_index("dp")
    e = lax.axis_index("expert")
    return d, e // 2, e % 2, e


def around(nd, d):
    if nd == 4:
        x, y = lax.rem(d, 2), d // 2
        near = [y * 2 + 1 - x, (1 - y) * 2 + x, 3 - d]
        return True, near, near
    return (
        False,
        [lax.rem(d + k, nd) for k in range(1, nd)],
        [lax.rem(d - k + nd, nd) for k in range(1, nd)],
    )


def enter(nd, nz, d, zz, c, e):
    barrier = pltpu.get_barrier_semaphore()
    peers = [(d, zz * 2 + 1 - c)]
    peers += [(lax.rem(d + k, nd), e) for k in range(1, nd)]
    peers += [(d, lax.rem(zz + i, nz) * 2 + c) for i in range(1, nz)]
    for pd, pe in peers:
        pl.semaphore_signal(barrier, inc=1, device_id={"dp": pd, "expert": pe}, device_id_type=MESH)
    pl.semaphore_wait(barrier, len(peers))


def remote(src, dst, send, recv, pd, pe):
    return pltpu.make_async_remote_copy(
        src_ref=src,
        dst_ref=dst,
        send_sem=send,
        recv_sem=recv,
        device_id={"dp": pd, "expert": pe},
        device_id_type=MESH,
    )


def gather_kernel(
    nd, nz, mv_ref, x_ref, rw_ref, id_ref, w_hbm, g_ref, got_hbm,
    out_ref, w_sem, a_send, a_recv, b_send, b_recv, c_send, c_recv, s_send, s_recv, *w_refs,
):
    d, zz, c, e = place(nd, nz)
    sibling = zz * 2 + 1 - c
    slots, parts, rows, _ = w_hbm.shape
    loads = [
        [pltpu.make_async_copy(w_hbm.at[j, m], w_refs[m].at[j], w_sem.at[j, m]) for j in range(slots)]
        for m in range(parts)
    ]
    for part in loads:
        for load in part:
            load.start()
    width = x_ref.shape[1]
    lanes = (g_ref.shape[4] - width) // 2
    lane = lax.broadcasted_iota(jnp.int32, (x_ref.shape[0], lanes), 1)
    share = jnp.zeros(lane.shape, jnp.float32)
    for k in range(id_ref.shape[1]):
        share += jnp.where(lane == id_ref[:, k : k + 1], rw_ref[:, k : k + 1], 0.0)
    high = share.astype(jnp.bfloat16)
    g_ref[c, zz, d, :, :width] = x_ref[...]
    g_ref[c, zz, d, :, width : width + lanes] = high
    g_ref[c, zz, d, :, width + lanes :] = (share - high.astype(jnp.float32)).astype(jnp.bfloat16)
    enter(nd, nz, d, zz, c, e)
    square, peers, origins = around(nd, d)
    started = []
    for i in range(1, nz):
        block = g_ref.at[c, zz, d]
        copy = remote(block, block, a_send.at[i - 1], a_recv.at[i - 1], d, lax.rem(zz + i, nz) * 2 + c)
        copy.start()
        started.append(copy)

    def to_dp(i):
        block = g_ref.at[c, lax.rem(zz - i + nz, nz), d]
        for k in range(1, 3 if square else nd):
            copy = remote(block, block, b_send.at[i, k - 1], b_recv.at[i, k - 1], peers[k - 1], e)
            copy.start()
            started.append(copy)

    def arrived(i, k):
        block = g_ref.at[c, lax.rem(zz - i + nz, nz), origins[k - 1]]
        remote(block, block, b_send.at[i, k - 1], b_recv.at[i, k - 1], d, e).wait_recv()

    def forward(i):
        if not square:
            return
        arrived(i, 1)
        arrived(i, 2)
        block = g_ref.at[c, lax.rem(zz - i + nz, nz), peers[i % 2]]
        copy = remote(block, block, b_send.at[i, 2], b_recv.at[i, 2], peers[1 - i % 2], e)
        copy.start()
        started.append(copy)

    to_dp(0)
    moving = mv_ref[e]
    tile = min(rows, 256)

    def swap(m):
        for load in loads[m]:
            load.wait()

        def step(r, carry):
            at = pl.ds(pl.multiple_of(r * tile, tile), tile)
            out_ref[m, at, :] = w_refs[m][moving, at, :]
            return carry

        lax.fori_loop(0, rows // tile, step, 0)
        copy = remote(out_ref.at[m], got_hbm.at[m], s_send.at[m], s_recv.at[m], d, sibling)
        copy.start()
        started.append(copy)
        return copy

    swaps = [swap(0)]
    for i in range(1, nz):
        block = g_ref.at[c, lax.rem(zz - i + nz, nz), d]
        remote(block, block, a_send.at[i - 1], a_recv.at[i - 1], d, e).wait_recv()
        to_dp(i)
        forward(i - 1)
        if i < parts:
            swaps.append(swap(i))
    forward(nz - 1)
    for m in range(max(1, nz), parts):
        swaps.append(swap(m))
    groups = []
    for i in range(nz):
        at = lax.rem(zz - i + nz, nz)
        for k in range(3 if square else 1, nd):
            arrived(i, k)
        copy = remote(g_ref.at[c, at], g_ref.at[c, at], c_send.at[i], c_recv.at[i], d, sibling)
        copy.start()
        started.append(copy)
        groups.append(copy)
    for copy in groups + swaps:
        copy.wait_recv()
    for copy in started:
        copy.wait_send()


def expert_kernel(
    place_ref, step_ref, mv_ref, g_ref, w_hbm, got_hbm, p_ref, moved_hbm,
    w_ref, x_ref, h_ref, m_ref, w_sem, m_sem, o_sem,
):
    blocks, rows_of, _ = g_ref.shape
    slots, parts, width, hidden = w_hbm.shape
    lanes = (g_ref.shape[2] - width) // 2
    chunk = min(width, 1024)
    chunks = width // chunk
    e = lax.axis_index("expert")

    def load(j, m, q):
        at = pl.ds(q * chunk, chunk)
        return pltpu.make_async_copy(w_hbm.at[j, m, at], w_ref.at[j, m, at], w_sem.at[j, m, q])

    order = [(j, m, q) for j in range(slots) for q in range(chunks) for m in (0, 1)]
    order += [(j, 2, q) for q in range(chunks) for j in range(slots)]
    for key in order:
        load(*key).start()
    first = e // 2 * 2
    swapping = step_ref[first] + step_ref[first + 1] > 0

    @pl.when(swapping)
    def _():
        for m in range(parts):
            pltpu.make_async_copy(got_hbm.at[m], m_ref.at[m], m_sem.at[m]).start()

    @pl.when(jnp.logical_not(swapping))
    def _():
        for m in range(parts):
            pltpu.make_async_copy(w_hbm.at[mv_ref[e], m], m_ref.at[m], m_sem.at[m]).start()

    def put(m):
        return pltpu.make_async_copy(m_ref.at[m], moved_hbm.at[0, m], o_sem.at[m])

    def put_all():
        for m in range(parts):
            pltpu.make_async_copy(got_hbm.at[m], m_ref.at[m], m_sem.at[m]).wait()
            put(m).start()

    per = min(blocks, max(1, 256 // rows_of))
    rows = per * rows_of

    def tile(t, waiting):
        at = pl.ds(t * per, per)
        x_ref[...] = g_ref[at, :, :width].astype(jnp.float32).reshape(rows, width).astype(jnp.bfloat16)
        share = (
            g_ref[at, :, width : width + lanes].astype(jnp.float32)
            + g_ref[at, :, width + lanes :].astype(jnp.float32)
        ).reshape(rows, lanes)
        lane = lax.broadcasted_iota(jnp.int32, (1, lanes), 1)
        held = jnp.full((1, lanes), -1, jnp.int32)
        for name in range(place_ref.shape[0]):
            held = jnp.where(lane == name, place_ref[name], held)
        for j in range(slots):
            weight = jnp.sum(jnp.where(held == e * slots + j, share, 0.0), axis=1, keepdims=True)
            gate = jnp.zeros((rows, hidden), jnp.float32)
            up = jnp.zeros((rows, hidden), jnp.float32)
            for q in range(chunks):
                cut = pl.ds(q * chunk, chunk)
                if waiting:
                    load(j, 0, q).wait()
                    load(j, 1, q).wait()
                x = x_ref[:, cut]
                gate += jnp.dot(x, w_ref[j, 0, cut, :], preferred_element_type=jnp.float32)
                up += jnp.dot(x, w_ref[j, 1, cut, :], preferred_element_type=jnp.float32)
            value = weight * (gate / (1.0 + jnp.exp(-gate)) * up)
            h_ref[:, pl.ds(j * hidden, hidden)] = value.astype(jnp.bfloat16)
        for q in range(chunks):
            if waiting and q == chunks // 2:
                put_all()
            cut = pl.ds(q * chunk, chunk)
            total = jnp.zeros((rows, chunk), jnp.float32)
            for j in range(slots):
                if waiting:
                    load(j, 2, q).wait()
                total += lax.dot_general(
                    h_ref[:, pl.ds(j * hidden, hidden)],
                    w_ref[j, 2, cut, :],
                    (((1,), (1,)), ((), ())),
                    preferred_element_type=jnp.float32,
                )
            p_ref[at, :, cut] = total.reshape(per, rows_of, chunk).astype(jnp.bfloat16)

    tile(0, True)
    if blocks > per:
        def step(t, carry):
            tile(t, False)
            return carry

        lax.fori_loop(1, blocks // per, step, 0)
    for m in range(parts):
        put(m).wait()


def scatter_kernel(
    nd, nz, p_ref, y_ref, rc_ref, s1_ref, rb_ref, s2_ref, ra_ref,
    a_send, a_recv, b_send, b_recv, c_send, c_recv,
):
    d, zz, c, e = place(nd, nz)
    sibling = zz * 2 + 1 - c
    f32 = jnp.float32
    enter(nd, nz, d, zz, c, e)
    started = []
    order = list(range(1, nz)) + [0]
    for i in order:
        at = lax.rem(zz + i, nz)
        copy = remote(p_ref.at[1 - c, at], rc_ref.at[i], c_send.at[i], c_recv.at[i], d, sibling)
        copy.start()
        started.append(copy)
    square, peers, origins = around(nd, d)

    def own(i, pd):
        return p_ref[c, lax.rem(zz + i, nz), pd].astype(f32) + rc_ref[i, pd].astype(f32)

    def send(i, k, src, dst, pd):
        copy = remote(src, dst, b_send.at[i, k], b_recv.at[i, k], pd, e)
        copy.start()
        started.append(copy)

    def arrived(i, k, dst):
        remote(dst, dst, b_send.at[i, k], b_recv.at[i, k], d, e).wait_recv()

    for i in order:
        at = lax.rem(zz + i, nz)
        remote(p_ref.at[1 - c, at], rc_ref.at[i], c_send.at[i], c_recv.at[i], d, sibling).wait_recv()
        if square:
            s1_ref[i, 0] = own(i, peers[i % 2]).astype(jnp.bfloat16)
            s1_ref[i, 1] = own(i, peers[2]).astype(jnp.bfloat16)
            send(i, 0, s1_ref.at[i, pl.ds(0, 2)], rb_ref.at[i, pl.ds(0, 2)], peers[i % 2])
            continue
        for k in range(1, nd):
            s1_ref[i, k - 1] = own(i, peers[k - 1]).astype(jnp.bfloat16)
            send(i, k - 1, s1_ref.at[i, k - 1], rb_ref.at[i, k - 1], peers[k - 1])
    if square:
        for i in order:
            arrived(i, 0, rb_ref.at[i, pl.ds(0, 2)])
            far = peers[1 - i % 2]
            s1_ref[i, 2] = (own(i, far) + rb_ref[i, 1].astype(f32)).astype(jnp.bfloat16)
            send(i, 1, s1_ref.at[i, 2], rb_ref.at[i, 2], far)
    final = None
    for i in order:
        total = own(i, d)
        if square:
            arrived(i, 1, rb_ref.at[i, 2])
            total += rb_ref[i, 0].astype(f32) + rb_ref[i, 2].astype(f32)
        else:
            for k in range(1, nd):
                arrived(i, k - 1, rb_ref.at[i, k - 1])
                total += rb_ref[i, k - 1].astype(f32)
        if i:
            s2_ref[i - 1] = total.astype(jnp.bfloat16)
            pe = lax.rem(zz + i, nz) * 2 + c
            copy = remote(s2_ref.at[i - 1], ra_ref.at[i - 1], a_send.at[i - 1], a_recv.at[i - 1], d, pe)
            copy.start()
            started.append(copy)
        else:
            final = total
    for i in range(1, nz):
        remote(s2_ref.at[i - 1], ra_ref.at[i - 1], a_send.at[i - 1], a_recv.at[i - 1], d, e).wait_recv()
        final += ra_ref[i - 1].astype(f32)
    y_ref[...] = final.astype(jnp.bfloat16)
    for copy in started:
        copy.wait_send()


def body(tokens, route_weight, expert_ids, placement, pair_step, move_slot, expert_weights):
    nd = lax.axis_size("dp")
    nz = lax.axis_size("expert") // 2
    e = lax.axis_index("expert")
    rows, width = tokens.shape
    slots, parts, _, hidden = expert_weights.shape
    bf16 = jnp.bfloat16
    vmem = pl.BlockSpec(memory_space=pltpu.VMEM)
    smem = pl.BlockSpec(memory_space=pltpu.SMEM)
    anywhere = pl.BlockSpec(memory_space=pl.ANY)
    dma = pltpu.SemaphoreType.DMA

    experts = placement.shape[0]
    full = width + 2 * (-(-experts // LANES) * LANES)

    gathered, got = pl.pallas_call(
        functools.partial(gather_kernel, nd, nz),
        out_shape=(
            jax.ShapeDtypeStruct((2, nz, nd, rows, full), bf16),
            jax.ShapeDtypeStruct((parts, width, hidden), bf16),
        ),
        in_specs=[smem, vmem, vmem, vmem, anywhere],
        out_specs=(vmem, anywhere),
        scratch_shapes=[
            pltpu.VMEM((parts, width, hidden), bf16),
            dma((slots, parts)),
            dma((nz - 1,)), dma((nz - 1,)),
            dma((nz, nd - 1)), dma((nz, nd - 1)),
            dma((nz,)), dma((nz,)),
            dma((parts,)), dma((parts,)),
        ] + [pltpu.VMEM((slots, width, hidden), bf16)] * parts,
        compiler_params=pltpu.CompilerParams(
            collective_id=0, has_side_effects=True, vmem_limit_bytes=VMEM_LIMIT
        ),
        name="gather",
    )(move_slot, tokens, route_weight, expert_ids, expert_weights)

    blocks = 2 * nz * nd
    per = min(blocks, max(1, 256 // rows))
    chunks = width // min(width, 1024)
    partial, moved = pl.pallas_call(
        expert_kernel,
        out_shape=(
            jax.ShapeDtypeStruct((blocks, rows, width), bf16),
            jax.ShapeDtypeStruct((1, parts, width, hidden), bf16),
        ),
        in_specs=[smem, smem, smem, vmem, anywhere, anywhere],
        out_specs=(vmem, anywhere),
        scratch_shapes=[
            pltpu.VMEM((slots, parts, width, hidden), bf16),
            pltpu.VMEM((per * rows, width), bf16),
            pltpu.VMEM((per * rows, slots * hidden), bf16),
            pltpu.VMEM((parts, width, hidden), bf16),
            dma((slots, parts, chunks)),
            dma((parts,)),
            dma((parts,)),
        ],
        compiler_params=pltpu.CompilerParams(vmem_limit_bytes=VMEM_LIMIT),
        name="experts",
    )(placement, pair_step, move_slot, gathered.reshape(blocks, rows, full), expert_weights, got)

    mixed = pl.pallas_call(
        functools.partial(scatter_kernel, nd, nz),
        out_shape=jax.ShapeDtypeStruct((rows, width), bf16),
        in_specs=[vmem],
        out_specs=vmem,
        scratch_shapes=[
            pltpu.VMEM((nz, nd, rows, width), bf16),
            pltpu.VMEM((nz, nd - 1, rows, width), bf16),
            pltpu.VMEM((nz, nd - 1, rows, width), bf16),
            pltpu.VMEM((nz - 1, rows, width), bf16),
            pltpu.VMEM((nz - 1, rows, width), bf16),
            dma((nz - 1,)), dma((nz - 1,)),
            dma((nz, nd - 1)), dma((nz, nd - 1)),
            dma((nz,)), dma((nz,)),
        ],
        compiler_params=pltpu.CompilerParams(
            collective_id=1, has_side_effects=True, vmem_limit_bytes=VMEM_LIMIT
        ),
        name="scatter",
    )(partial.reshape(2, nz, nd, rows, width))
    return mixed, moved


def solution(mesh):
    in_specs = (
        P(("dp", "expert"), None),
        P(("dp", "expert"), None),
        P(("dp", "expert"), None),
        P(),
        P(),
        P(),
        P("expert", None, None, "dp"),
    )
    out_specs = (P(("dp", "expert"), None), P("expert", None, None, "dp"))
    return jax.shard_map(body, mesh=mesh, in_specs=in_specs, out_specs=out_specs, check_vma=False)
```

```python
import functools

import jax
import jax.numpy as jnp
from jax import lax
from jax.experimental import pallas as pl
from jax.experimental.pallas import tpu as pltpu
from jax.sharding import PartitionSpec as P

MESH = pl.DeviceIdType.MESH
LANES = 128
VMEM_LIMIT = 56 * 1024 * 1024


def place(nd, nz):
    d = lax.axis_index("dp")
    e = lax.axis_index("expert")
    return d, e // 2, e % 2, e


def enter(nd, nz, d, zz, c, e):
    barrier = pltpu.get_barrier_semaphore()
    peers = [(d, zz * 2 + 1 - c)]
    peers += [(lax.rem(d + k, nd), e) for k in range(1, nd)]
    peers += [(d, lax.rem(zz + i, nz) * 2 + c) for i in range(1, nz)]
    for pd, pe in peers:
        pl.semaphore_signal(barrier, inc=1, device_id={"dp": pd, "expert": pe}, device_id_type=MESH)
    pl.semaphore_wait(barrier, len(peers))


def remote(src, dst, send, recv, pd, pe):
    return pltpu.make_async_remote_copy(
        src_ref=src,
        dst_ref=dst,
        send_sem=send,
        recv_sem=recv,
        device_id={"dp": pd, "expert": pe},
        device_id_type=MESH,
    )


def layer_kernel(
    nd, nz, place_ref, step_ref, mv_ref, x_ref, rw_ref, id_ref, w_hbm, y_ref, moved_hbm,
    g_ref, t_ref, h_ref, out_ref, got_ref, rc_ref, rb_ref, s2_ref, ra_ref, *rest,
):
    d, zz, c, e = place(nd, nz)
    sibling = zz * 2 + 1 - c
    f32, bf16 = jnp.float32, jnp.bfloat16
    slots, parts, width, hidden = w_hbm.shape
    w_refs = rest[:parts]
    (w_sem, o_sem, s_send, s_recv, a_send, a_recv, b_send, b_recv, c_send, c_recv,
     ra_send, ra_recv, rb_send, rb_recv, rc_send, rc_recv) = rest[parts:]
    tokens, lanes = x_ref.shape[0], (g_ref.shape[3] - width) // 2
    loads = [
        [pltpu.make_async_copy(w_hbm.at[j, m], w_refs[m].at[j], w_sem.at[j, m]) for j in range(slots)]
        for m in range(parts)
    ]
    for part in loads:
        for load in part:
            load.start()
    lane = lax.broadcasted_iota(jnp.int32, (tokens, lanes), 1)
    share = jnp.zeros(lane.shape, f32)
    for k in range(id_ref.shape[1]):
        share += jnp.where(lane == id_ref[:, k : k + 1], rw_ref[:, k : k + 1], 0.0)
    high = share.astype(bf16)
    mine = zz * nd + d
    g_ref[c, mine, :, :width] = x_ref[...]
    g_ref[c, mine, :, width : width + lanes] = high
    g_ref[c, mine, :, width + lanes :] = (share - high.astype(f32)).astype(bf16)
    enter(nd, nz, d, zz, c, e)

    sent = []

    def send(src, dst, send_sem, recv_sem, pd, pe):
        copy = remote(src, dst, send_sem, recv_sem, pd, pe)
        copy.start()
        sent.append(copy)

    def arrived(dst, recv_sem):
        remote(dst, dst, recv_sem, recv_sem, d, sibling).wait_recv()

    def line(i):
        return lax.rem(zz - i + nz, nz)

    for i in range(1, nz):
        block = g_ref.at[c, mine]
        send(block, block, a_send.at[i - 1], a_recv.at[i - 1], d, lax.rem(zz + i, nz) * 2 + c)

    def to_dp(i):
        block = g_ref.at[c, line(i) * nd + d]
        for k in range(1, nd):
            send(block, block, b_send.at[i, k - 1], b_recv.at[i, k - 1], lax.rem(d + k, nd), e)

    to_dp(0)
    moving = mv_ref[e]
    tall = min(width, 256)
    swaps = []

    def rows_loop(fn):
        def step(r, carry):
            fn(pl.ds(pl.multiple_of(r * tall, tall), tall))
            return carry

        lax.fori_loop(0, width // tall, step, 0)

    def swap(m):
        for load in loads[m]:
            load.wait()

        def one(at):
            out_ref[m, at, :] = w_refs[m][moving, at, :]

        rows_loop(one)
        copy = remote(out_ref.at[m], got_ref.at[m], s_send.at[m], s_recv.at[m], d, sibling)
        copy.start()
        swaps.append(copy)

    swap(0)
    for i in range(1, nz):
        arrived(g_ref.at[c, line(i) * nd + d], a_recv.at[i - 1])
        to_dp(i)
    for m in range(1, parts):
        swap(m)
    for i in range(nz):
        for k in range(1, nd):
            arrived(g_ref.at[c, line(i) * nd + lax.rem(d - k + nd, nd)], b_recv.at[i, k - 1])
        group = pl.ds(line(i) * nd, nd)
        send(g_ref.at[c, group], g_ref.at[c, group], c_send.at[i], c_recv.at[i], d, sibling)

    blocks = nz * nd
    per = min(blocks, max(1, 256 // tokens))
    rows = per * tokens
    row = lax.broadcasted_iota(jnp.int32, (1, lanes), 1)
    held = jnp.full((1, lanes), -1, jnp.int32)
    for name in range(place_ref.shape[0]):
        held = jnp.where(row == name, place_ref[name], held)

    def each(fn):
        if blocks == per:
            fn(0)
            return

        def step(t, carry):
            fn(t)
            return carry

        lax.fori_loop(0, blocks // per, step, 0)

    chunk = min(width, 1024)

    def gate_up(half):
        def one(t):
            at = pl.ds(t * per, per)
            t_ref[...] = g_ref[half, at, :, :width].astype(f32).reshape(rows, width).astype(bf16)
            part = (
                g_ref[half, at, :, width : width + lanes].astype(f32)
                + g_ref[half, at, :, width + lanes :].astype(f32)
            ).reshape(rows, lanes)
            for j in range(slots):
                weight = jnp.sum(jnp.where(held == e * slots + j, part, 0.0), axis=1, keepdims=True)
                gate = jnp.zeros((rows, hidden), f32)
                up = jnp.zeros((rows, hidden), f32)
                for q in range(0, width, chunk):
                    x = t_ref[:, q : q + chunk]
                    gate += jnp.dot(x, w_refs[0][j, q : q + chunk, :], preferred_element_type=f32)
                    up += jnp.dot(x, w_refs[1][j, q : q + chunk, :], preferred_element_type=f32)
                value = weight * (gate / (1.0 + jnp.exp(-gate)) * up)
                h_ref[half, pl.ds(t * rows, rows), j * hidden : (j + 1) * hidden] = value.astype(bf16)

        each(one)

    def down(half):
        def one(t):
            at = pl.ds(t * per, per)
            for q in range(0, width, chunk):
                total = jnp.zeros((rows, chunk), f32)
                for j in range(slots):
                    total += lax.dot_general(
                        h_ref[half, pl.ds(t * rows, rows), j * hidden : (j + 1) * hidden],
                        w_refs[2][j, q : q + chunk, :],
                        (((1,), (1,)), ((), ())),
                        preferred_element_type=f32,
                    )
                g_ref[half, at, :, q : q + chunk] = total.reshape(per, tokens, chunk).astype(bf16)

        each(one)

    gate_up(c)
    for i in range(nz):
        arrived(g_ref.at[1 - c, pl.ds(line(i) * nd, nd)], c_recv.at[i])
    gate_up(1 - c)
    for copy in sent:
        copy.wait_send()
    sent.clear()
    down(1 - c)

    order = list(range(1, nz)) + [0]

    def ahead(i):
        return lax.rem(zz + i, nz)

    def p_view(half, at):
        return g_ref.at[half, pl.ds(at * nd, nd), :, pl.ds(0, width)]

    for i in order:
        send(p_view(1 - c, ahead(i)), rc_ref.at[i], rc_send.at[i], rc_recv.at[i], d, sibling)
    down(c)
    for i in order:
        arrived(rc_ref.at[i], rc_recv.at[i])
        for k in list(range(1, nd)) + [0]:
            pd = lax.rem(d + k, nd)
            rc_ref[i, pd] = (g_ref[c, ahead(i) * nd + pd, :, :width].astype(f32) + rc_ref[i, pd].astype(f32)).astype(bf16)
            if k:
                send(rc_ref.at[i, pd], rb_ref.at[i, k - 1], rb_send.at[i, k - 1], rb_recv.at[i, k - 1], pd, e)
    first = e // 2 * 2
    swapping = step_ref[first] + step_ref[first + 1] > 0
    puts = []
    for m in range(parts):
        swaps[m].wait_recv()

        def one(at):
            got_ref[m, at, :] = lax.select(swapping, got_ref[m, at, :], out_ref[m, at, :])

        rows_loop(one)
        put = pltpu.make_async_copy(got_ref.at[m], moved_hbm.at[0, m], o_sem.at[m])
        put.start()
        puts.append(put)
    final = None
    for i in order:
        total = rc_ref[i, d].astype(f32)
        for k in range(1, nd):
            arrived(rb_ref.at[i, k - 1], rb_recv.at[i, k - 1])
            total += rb_ref[i, k - 1].astype(f32)
        if i:
            s2_ref[i - 1] = total.astype(bf16)
            send(s2_ref.at[i - 1], ra_ref.at[i - 1], ra_send.at[i - 1], ra_recv.at[i - 1], d, ahead(i) * 2 + c)
        else:
            final = total
    for i in range(1, nz):
        arrived(ra_ref.at[i - 1], ra_recv.at[i - 1])
        final += ra_ref[i - 1].astype(f32)
    y_ref[...] = final.astype(bf16)
    for copy in sent + swaps:
        copy.wait_send()
    for put in puts:
        put.wait()


def body(tokens, route_weight, expert_ids, placement, pair_step, move_slot, expert_weights):
    nd = lax.axis_size("dp")
    nz = lax.axis_size("expert") // 2
    rows, width = tokens.shape
    slots, parts, _, hidden = expert_weights.shape
    bf16 = jnp.bfloat16
    vmem = pl.BlockSpec(memory_space=pltpu.VMEM)
    smem = pl.BlockSpec(memory_space=pltpu.SMEM)
    anywhere = pl.BlockSpec(memory_space=pl.ANY)
    dma = pltpu.SemaphoreType.DMA
    experts = placement.shape[0]
    full = width + 2 * (-(-experts // LANES) * LANES)
    blocks = nz * nd
    per = min(blocks, max(1, 256 // rows))
    return pl.pallas_call(
        functools.partial(layer_kernel, nd, nz),
        out_shape=(
            jax.ShapeDtypeStruct((rows, width), bf16),
            jax.ShapeDtypeStruct((1, parts, width, hidden), bf16),
        ),
        in_specs=[smem, smem, smem, vmem, vmem, vmem, anywhere],
        out_specs=(vmem, anywhere),
        scratch_shapes=[
            pltpu.VMEM((2, blocks, rows, full), bf16),
            pltpu.VMEM((per * rows, width), bf16),
            pltpu.VMEM((2, blocks * rows, slots * hidden), bf16),
            pltpu.VMEM((parts, width, hidden), bf16),
            pltpu.VMEM((parts, width, hidden), bf16),
            pltpu.VMEM((nz, nd, rows, width), bf16),
            pltpu.VMEM((nz, nd - 1, rows, width), bf16),
            pltpu.VMEM((nz - 1, rows, width), bf16),
            pltpu.VMEM((nz - 1, rows, width), bf16),
        ]
        + [pltpu.VMEM((slots, width, hidden), bf16)] * parts
        + [dma((slots, parts)), dma((parts,)), dma((parts,)), dma((parts,))]
        + [dma((nz - 1,))] * 2 + [dma((nz, nd - 1))] * 2 + [dma((nz,))] * 2
        + [dma((nz - 1,))] * 2 + [dma((nz, nd - 1))] * 2 + [dma((nz,))] * 2,
        compiler_params=pltpu.CompilerParams(
            collective_id=0, has_side_effects=True, vmem_limit_bytes=VMEM_LIMIT
        ),
        name="layer",
    )(placement, pair_step, move_slot, tokens, route_weight, expert_ids, expert_weights)


def solution(mesh):
    in_specs = (
        P(("dp", "expert"), None),
        P(("dp", "expert"), None),
        P(("dp", "expert"), None),
        P(),
        P(),
        P(),
        P("expert", None, None, "dp"),
    )
    out_specs = (P(("dp", "expert"), None), P("expert", None, None, "dp"))
    return jax.shard_map(body, mesh=mesh, in_specs=in_specs, out_specs=out_specs, check_vma=False)
```

```python
import functools

import jax
import jax.numpy as jnp
from jax import lax
from jax.experimental import pallas as pl
from jax.experimental.pallas import tpu as pltpu
from jax.sharding import PartitionSpec as P

MESH = pl.DeviceIdType.MESH
LANES = 128
VMEM_LIMIT = 52 * 1024 * 1024


def place(nd, nz):
    d = lax.axis_index("dp")
    e = lax.axis_index("expert")
    return d, e // 2, e % 2, e


def enter(nd, nz, d, zz, c, e):
    barrier = pltpu.get_barrier_semaphore()
    peers = [(d, zz * 2 + 1 - c)]
    peers += [(lax.rem(d + k, nd), e) for k in range(1, nd)]
    peers += [(d, lax.rem(zz + i, nz) * 2 + c) for i in range(1, nz)]
    for pd, pe in peers:
        pl.semaphore_signal(barrier, inc=1, device_id={"dp": pd, "expert": pe}, device_id_type=MESH)
    pl.semaphore_wait(barrier, len(peers))


def remote(src, dst, send, recv, pd, pe):
    return pltpu.make_async_remote_copy(
        src_ref=src,
        dst_ref=dst,
        send_sem=send,
        recv_sem=recv,
        device_id={"dp": pd, "expert": pe},
        device_id_type=MESH,
    )


def layer_kernel(
    nd, nz, place_ref, step_ref, mv_ref, x_ref, rw_ref, id_ref, w_hbm, y_ref, moved_ref,
    g_ref, t_ref, h_ref, out_ref, got_ref, rc_ref, rb_ref, s2_ref, ra_ref, *rest,
):
    d, zz, c, e = place(nd, nz)
    sibling = zz * 2 + 1 - c
    f32, bf16 = jnp.float32, jnp.bfloat16
    slots, parts, width, hidden = w_hbm.shape
    w_refs = rest[:parts]
    (w_sem, s_send, s_recv, a_send, a_recv, b_send, b_recv, c_send, c_recv,
     ra_send, ra_recv, rb_send, rb_recv, rc_send, rc_recv) = rest[parts:]
    tokens, lanes = x_ref.shape[0], (g_ref.shape[3] - width) // 2
    loads = [
        [pltpu.make_async_copy(w_hbm.at[j, m], w_refs[m].at[j], w_sem.at[j, m]) for j in range(slots)]
        for m in range(parts)
    ]
    for part in loads:
        for load in part:
            load.start()
    lane = lax.broadcasted_iota(jnp.int32, (tokens, lanes), 1)
    share = jnp.zeros(lane.shape, f32)
    for k in range(id_ref.shape[1]):
        share += jnp.where(lane == id_ref[:, k : k + 1], rw_ref[:, k : k + 1], 0.0)
    high = share.astype(bf16)
    mine = zz * nd + d
    g_ref[c, mine, :, :width] = x_ref[...]
    g_ref[c, mine, :, width : width + lanes] = high
    g_ref[c, mine, :, width + lanes :] = (share - high.astype(f32)).astype(bf16)
    enter(nd, nz, d, zz, c, e)

    sent = []

    def send(src, dst, send_sem, recv_sem, pd, pe):
        copy = remote(src, dst, send_sem, recv_sem, pd, pe)
        copy.start()
        sent.append(copy)

    def arrived(dst, recv_sem):
        remote(dst, dst, recv_sem, recv_sem, d, sibling).wait_recv()

    def line(i):
        return lax.rem(zz - i + nz, nz)

    for i in range(1, nz):
        block = g_ref.at[c, mine]
        send(block, block, a_send.at[i - 1], a_recv.at[i - 1], d, lax.rem(zz + i, nz) * 2 + c)

    def to_dp(i):
        block = g_ref.at[c, line(i) * nd + d]
        for k in range(1, nd):
            send(block, block, b_send.at[i, k - 1], b_recv.at[i, k - 1], lax.rem(d + k, nd), e)

    to_dp(0)
    moving = mv_ref[e]
    tall = min(width, 256)
    swaps = []

    def rows_loop(fn):
        def step(r, carry):
            fn(pl.ds(pl.multiple_of(r * tall, tall), tall))
            return carry

        lax.fori_loop(0, width // tall, step, 0)

    def swap(m):
        for load in loads[m]:
            load.wait()

        def one(at):
            out_ref[m, at, :] = w_refs[m][moving, at, :]

        rows_loop(one)
        copy = remote(out_ref.at[m], got_ref.at[m], s_send.at[m], s_recv.at[m], d, sibling)
        copy.start()
        swaps.append(copy)

    swap(0)
    for i in range(1, nz):
        arrived(g_ref.at[c, line(i) * nd + d], a_recv.at[i - 1])
        to_dp(i)
    for m in range(1, parts):
        swap(m)
    for i in range(nz):
        for k in range(1, nd):
            arrived(g_ref.at[c, line(i) * nd + lax.rem(d - k + nd, nd)], b_recv.at[i, k - 1])
        group = pl.ds(line(i) * nd, nd)
        send(g_ref.at[c, group], g_ref.at[c, group], c_send.at[i], c_recv.at[i], d, sibling)

    blocks = nz * nd
    per = min(blocks, max(1, 256 // tokens))
    rows = per * tokens
    row = lax.broadcasted_iota(jnp.int32, (1, lanes), 1)
    held = jnp.full((1, lanes), -1, jnp.int32)
    for name in range(place_ref.shape[0]):
        held = jnp.where(row == name, place_ref[name], held)

    def each(fn):
        if blocks == per:
            fn(0)
            return

        def step(t, carry):
            fn(t)
            return carry

        lax.fori_loop(0, blocks // per, step, 0)

    chunk = min(width, 1024)

    def gate_up(half):
        def one(t):
            at = pl.ds(t * per, per)
            t_ref[...] = g_ref[half, at, :, :width].astype(f32).reshape(rows, width).astype(bf16)
            part = (
                g_ref[half, at, :, width : width + lanes].astype(f32)
                + g_ref[half, at, :, width + lanes :].astype(f32)
            ).reshape(rows, lanes)
            for j in range(slots):
                weight = jnp.sum(jnp.where(held == e * slots + j, part, 0.0), axis=1, keepdims=True)
                gate = jnp.zeros((rows, hidden), f32)
                up = jnp.zeros((rows, hidden), f32)
                for q in range(0, width, chunk):
                    x = t_ref[:, q : q + chunk]
                    gate += jnp.dot(x, w_refs[0][j, q : q + chunk, :], preferred_element_type=f32)
                    up += jnp.dot(x, w_refs[1][j, q : q + chunk, :], preferred_element_type=f32)
                value = weight * (gate / (1.0 + jnp.exp(-gate)) * up)
                h_ref[half, pl.ds(t * rows, rows), j * hidden : (j + 1) * hidden] = value.astype(bf16)

        each(one)

    def down(half):
        def one(t):
            at = pl.ds(t * per, per)
            for q in range(0, width, chunk):
                total = jnp.zeros((rows, chunk), f32)
                for j in range(slots):
                    total += lax.dot_general(
                        h_ref[half, pl.ds(t * rows, rows), j * hidden : (j + 1) * hidden],
                        w_refs[2][j, q : q + chunk, :],
                        (((1,), (1,)), ((), ())),
                        preferred_element_type=f32,
                    )
                g_ref[half, at, :, q : q + chunk] = total.reshape(per, tokens, chunk).astype(bf16)

        each(one)

    gate_up(c)
    for i in range(nz):
        arrived(g_ref.at[1 - c, pl.ds(line(i) * nd, nd)], c_recv.at[i])
    gate_up(1 - c)
    for copy in sent:
        copy.wait_send()
    sent.clear()
    down(1 - c)

    order = list(range(1, nz)) + [0]

    def ahead(i):
        return lax.rem(zz + i, nz)

    def p_view(half, at):
        return g_ref.at[half, pl.ds(at * nd, nd), :, pl.ds(0, width)]

    for i in order:
        send(p_view(1 - c, ahead(i)), rc_ref.at[i], rc_send.at[i], rc_recv.at[i], d, sibling)
    down(c)
    for i in order:
        arrived(rc_ref.at[i], rc_recv.at[i])
        for k in list(range(1, nd)) + [0]:
            pd = lax.rem(d + k, nd)
            rc_ref[i, pd] = (g_ref[c, ahead(i) * nd + pd, :, :width].astype(f32) + rc_ref[i, pd].astype(f32)).astype(bf16)
            if k:
                send(rc_ref.at[i, pd], rb_ref.at[i, k - 1], rb_send.at[i, k - 1], rb_recv.at[i, k - 1], pd, e)
    first = e // 2 * 2
    swapping = step_ref[first] + step_ref[first + 1] > 0
    for m in range(parts):
        swaps[m].wait_recv()

        def one(at):
            moved_ref[0, m, at, :] = lax.select(swapping, got_ref[m, at, :], out_ref[m, at, :])

        rows_loop(one)
    final = None
    for i in order:
        total = rc_ref[i, d].astype(f32)
        for k in range(1, nd):
            arrived(rb_ref.at[i, k - 1], rb_recv.at[i, k - 1])
            total += rb_ref[i, k - 1].astype(f32)
        if i:
            s2_ref[i - 1] = total.astype(bf16)
            send(s2_ref.at[i - 1], ra_ref.at[i - 1], ra_send.at[i - 1], ra_recv.at[i - 1], d, ahead(i) * 2 + c)
        else:
            final = total
    for i in range(1, nz):
        arrived(ra_ref.at[i - 1], ra_recv.at[i - 1])
        final += ra_ref[i - 1].astype(f32)
    y_ref[...] = final.astype(bf16)
    for copy in sent + swaps:
        copy.wait_send()


def body(tokens, route_weight, expert_ids, placement, pair_step, move_slot, expert_weights):
    nd = lax.axis_size("dp")
    nz = lax.axis_size("expert") // 2
    rows, width = tokens.shape
    slots, parts, _, hidden = expert_weights.shape
    bf16 = jnp.bfloat16
    vmem = pl.BlockSpec(memory_space=pltpu.VMEM)
    smem = pl.BlockSpec(memory_space=pltpu.SMEM)
    anywhere = pl.BlockSpec(memory_space=pl.ANY)
    dma = pltpu.SemaphoreType.DMA
    experts = placement.shape[0]
    full = width + 2 * (-(-experts // LANES) * LANES)
    blocks = nz * nd
    per = min(blocks, max(1, 256 // rows))
    return pl.pallas_call(
        functools.partial(layer_kernel, nd, nz),
        out_shape=(
            jax.ShapeDtypeStruct((rows, width), bf16),
            pltpu.VMEM((1, parts, width, hidden), bf16),
        ),
        in_specs=[smem, smem, smem, vmem, vmem, vmem, anywhere],
        out_specs=(vmem, vmem),
        scratch_shapes=[
            pltpu.VMEM((2, blocks, rows, full), bf16),
            pltpu.VMEM((per * rows, width), bf16),
            pltpu.VMEM((2, blocks * rows, slots * hidden), bf16),
            pltpu.VMEM((parts, width, hidden), bf16),
            pltpu.VMEM((parts, width, hidden), bf16),
            pltpu.VMEM((nz, nd, rows, width), bf16),
            pltpu.VMEM((nz, nd - 1, rows, width), bf16),
            pltpu.VMEM((nz - 1, rows, width), bf16),
            pltpu.VMEM((nz - 1, rows, width), bf16),
        ]
        + [pltpu.VMEM((slots, width, hidden), bf16)] * parts
        + [dma((slots, parts)), dma((parts,)), dma((parts,))]
        + [dma((nz - 1,))] * 2 + [dma((nz, nd - 1))] * 2 + [dma((nz,))] * 2
        + [dma((nz - 1,))] * 2 + [dma((nz, nd - 1))] * 2 + [dma((nz,))] * 2,
        compiler_params=pltpu.CompilerParams(
            collective_id=0, has_side_effects=True, vmem_limit_bytes=VMEM_LIMIT
        ),
        name="layer",
    )(placement, pair_step, move_slot, tokens, route_weight, expert_ids, expert_weights)


def solution(mesh):
    in_specs = (
        P(("dp", "expert"), None),
        P(("dp", "expert"), None),
        P(("dp", "expert"), None),
        P(),
        P(),
        P(),
        P("expert", None, None, "dp"),
    )
    out_specs = (P(("dp", "expert"), None), P("expert", None, None, "dp"))
    return jax.shard_map(body, mesh=mesh, in_specs=in_specs, out_specs=out_specs, check_vma=False)
```
